32 devices in a mesh: freq: 4 (over y, x), space: 8 (over z, core).
Axes of the slice: x: 2, y: 2, z: 4, core: 2. Of those that a mesh axis runs over, the one named last changes fastest.
Arguments:
- spectra: bfloat16 [2, 256, 24, 32768], P(None, 'freq', None, 'space'), may hold values from -6 to 6
- eigvecs: bfloat16 [2, 256, 4, 32768], P(None, 'freq', None, 'space'), may hold values from -6 to 6
- weights: bfloat16 [32768], P('space'), may hold values from 0.19921875 to 5
Outputs:
- filtered: float32 [3200, 32768], P(None, ('space', 'freq'))
The draws below stay inside these ranges and needn't reach their ends.
All inputs are finite; a program needn't handle non-finite values.
Results may differ from the reference program's by a relative error of at most 0.004.
Values may be sent and summed in bfloat16 or wider, within the bound.
A program may use at most 128 MiB of HBM per device.

```python
import math
import jax
import jax.numpy as jnp
from jax import lax

NFREQ = 256
MODES = 4
BLOCKS = 24
P_DEV = 4096
POINTS = 32768
TIME = 3200
N_SPACE = 8


def level_of(rng, shape, split, smallest, top_value):
    factor_of, own = 1.0, jax.random.fold_in(rng, 6)
    for position, parts in split:
        heights = jnp.exp(jax.random.uniform(jax.random.fold_in(own, position), (parts,), jnp.float32, smallest / len(split), top_value / len(split)))
        factor_of = factor_of * jnp.repeat(heights, shape[position] // parts).reshape([-1 if axis == position else 1 for axis in range(len(shape))])
    return factor_of


def gaussian(rng, extent, deviation, limit, split=(), kind=jnp.bfloat16):
    drawn = deviation * jax.random.normal(rng, extent, jnp.float32)
    if split:
        drawn = drawn * level_of(rng, extent, split, -0.22, 0.18)
    return jnp.clip(drawn, -limit, limit).astype(kind)


def setup_inputs(seed: int = 0) -> dict:
    splits = jax.random.split(jax.random.key(seed), 4)
    spectra = gaussian(splits[0], (2, NFREQ, BLOCKS, POINTS), 1.0, 6.0, ((1, 4), (3, 8)))
    eigvecs = gaussian(splits[1], (2, NFREQ, MODES, POINTS), 1.0, 6.0, ((1, 4), (3, 8)))
    weights = jnp.clip(jnp.exp(math.log(5.0) - 3.2227897 * jax.random.uniform(splits[2], (POINTS,), jnp.float32) ** level_of(splits[2], (POINTS,), ((0, 8),), -0.2, 0.2)), 0.19921875, 5.0).astype(jnp.bfloat16)
    return dict(spectra=spectra, eigvecs=eigvecs, weights=weights)


def coefficient_terms(spectra_block, weighted_block):
    spectra_real = spectra_block[0].astype(jnp.float32)
    spectra_imag = spectra_block[1].astype(jnp.float32)
    modes_real = weighted_block[0].astype(jnp.float32)
    modes_imag = weighted_block[1].astype(jnp.float32)
    highest = lax.Precision.HIGHEST
    real_terms = jnp.einsum('kmp,kbp->kbm', modes_real, spectra_real, precision=highest) + jnp.einsum('kmp,kbp->kbm', modes_imag, spectra_imag, precision=highest)
    imag_terms = jnp.einsum('kmp,kbp->kbm', modes_real, spectra_imag, precision=highest) - jnp.einsum('kmp,kbp->kbm', modes_imag, spectra_real, precision=highest)
    return jnp.stack([real_terms, imag_terms])

def rebuild(modes_block, coefficients):
    highest = lax.Precision.HIGHEST
    modes_real = modes_block[0].astype(jnp.float32)
    modes_imag = modes_block[1].astype(jnp.float32)
    coef_real = coefficients[0]
    coef_imag = coefficients[1]
    real_part = jnp.einsum('kmp,kbm->kbp', modes_real, coef_real, precision=highest) - jnp.einsum('kmp,kbm->kbp', modes_imag, coef_imag, precision=highest)
    imag_part = jnp.einsum('kmp,kbm->kbp', modes_real, coef_imag, precision=highest) + jnp.einsum('kmp,kbm->kbp', modes_imag, coef_real, precision=highest)
    return jnp.stack([real_part, imag_part]).astype(jnp.bfloat16)

def correlation_add(series):
    length = series.shape[0]
    half_length = length // 2
    window = jnp.sin(math.pi * (jnp.arange(length, dtype=jnp.float32) + 0.5) / length)
    shaped = (series * window[:, None, None]).reshape(2, half_length, series.shape[1], series.shape[2])
    zeros_block = jnp.zeros((half_length, 1, series.shape[2]), jnp.float32)
    leading = jnp.concatenate([shaped[0], zeros_block], axis=1)
    trailing = jnp.concatenate([zeros_block, shaped[1]], axis=1)
    summed = leading + trailing
    return jnp.transpose(summed, (1, 0, 2)).reshape(-1, series.shape[2])

def reference(spectra, eigvecs, weights):
    weighted = (eigvecs.astype(jnp.float32) * weights.astype(jnp.float32)).astype(jnp.bfloat16)
    factor = 1.0 / math.sqrt(POINTS)

    def partial_sum(index):
        start = (index * P_DEV).astype(jnp.int32)
        return coefficient_terms(lax.dynamic_slice_in_dim(spectra, start, P_DEV, 3), lax.dynamic_slice_in_dim(weighted, start, P_DEV, 3))
    indices = jnp.arange(N_SPACE, dtype=jnp.int32)
    coefficients = lax.optimization_barrier(jnp.sum(lax.map(partial_sum, indices), axis=0)) * factor

    def filtered_block(index):
        start = (index * P_DEV).astype(jnp.int32)
        rebuilt = rebuild(lax.dynamic_slice_in_dim(eigvecs, start, P_DEV, 3), coefficients).astype(jnp.float32)
        series = jnp.fft.ifft(rebuilt[0] + 1j * rebuilt[1], axis=0).real * math.sqrt(NFREQ)
        return correlation_add(series)
    pieces = lax.map(filtered_block, indices)
    return jnp.transpose(pieces, (1, 0, 2)).reshape(TIME, POINTS)
```

```python
import functools
import math

import jax
import jax.numpy as jnp
import numpy as np
from jax import lax
from jax.experimental import pallas as pl
from jax.experimental.pallas import tpu as pltpu
from jax.sharding import PartitionSpec as P

MESH = pl.DeviceIdType.MESH
GROUP = 32


def project_kernel(blocks, group, modes_ref, spectra_ref, weights_ref, out_ref, acc_ref):
    step = pl.program_id(1)
    half = modes_ref.shape[2]
    weights = weights_ref[...].astype(jnp.float32)
    weighted = jnp.concatenate(
        [(modes_ref[0, c].astype(jnp.float32) * weights).astype(jnp.bfloat16) for c in range(2)], axis=0
    )
    owner = lax.broadcasted_iota(jnp.int32, (blocks, 2 * half), 1) % half // (half // group)

    @pl.when(step == 0)
    def _():
        acc_ref[...] = jnp.zeros_like(acc_ref)

    for c in range(2):
        product = lax.dot_general(
            spectra_ref[c], weighted, (((1,), (1,)), ((), ())), preferred_element_type=jnp.float32
        )
        total = acc_ref[c]
        for j in range(group):
            total += jnp.where(owner == j, product[j * blocks : (j + 1) * blocks], 0.0)
        acc_ref[c] = total

    @pl.when(step == pl.num_programs(1) - 1)
    def _():
        out_ref[0, 0] = acc_ref[0][:, :half] + acc_ref[1][:, half:]
        out_ref[0, 1] = acc_ref[1][:, :half] - acc_ref[0][:, half:]


def project(modes, spectra, weights, blocks, group, modes_count):
    parts, _, rows, width = modes.shape
    half = group * modes_count
    steps = rows // half
    points = spectra.shape[2]
    return pl.pallas_call(
        functools.partial(project_kernel, blocks, group),
        out_shape=jax.ShapeDtypeStruct((steps, 2, blocks, half), jnp.float32),
        grid=(steps, parts),
        in_specs=[
            pl.BlockSpec((1, 2, half, width), lambda h, i: (i, 0, h, 0)),
            pl.BlockSpec((2, group * blocks, width), lambda h, i: (0, h, i)),
            pl.BlockSpec((1, width), lambda h, i: (0, i)),
        ],
        out_specs=pl.BlockSpec((1, 2, blocks, half), lambda h, i: (h, 0, 0, 0)),
        scratch_shapes=[pltpu.VMEM((2, blocks, 2 * half), jnp.float32)],
        compiler_params=pltpu.CompilerParams(vmem_limit_bytes=48 << 20),
        cost_estimate=pl.CostEstimate(
            flops=4 * spectra.shape[1] * points * 2 * half,
            bytes_accessed=4 * spectra.shape[1] * points,
            transcendentals=0,
        ),
        name="project",
    )(modes, spectra, weights)


def exchange_kernel(n_freq, n_space, part_ref, out_ref, land, own, every, send1, recv1, send2, recv2):
    f = lax.axis_index("freq")
    s = lax.axis_index("space")
    peers = [(df, ds) for df in range(n_freq) for ds in range(n_space) if (df, ds) != (0, 0)]

    def at(df, ds):
        return (lax.rem(f + df, n_freq), lax.rem(s + ds, n_space))

    barrier = pltpu.get_barrier_semaphore()
    for df, ds in peers:
        pl.semaphore_signal(barrier, inc=1, device_id=at(df, ds), device_id_type=MESH)
    pl.semaphore_wait(barrier, len(peers))

    first = []
    for ds in range(1, n_space):
        target = at(0, ds)
        copy = pltpu.make_async_remote_copy(
            src_ref=part_ref.at[target[1]], dst_ref=land.at[ds],
            send_sem=send1.at[ds], recv_sem=recv1.at[ds],
            device_id=target, device_id_type=MESH,
        )
        copy.start()
        first.append(copy)
    total = part_ref[s]
    for ds in range(1, n_space):
        first[ds - 1].wait_recv()
        total += land[ds]
    own[...] = total
    second = []
    for df, ds in peers:
        copy = pltpu.make_async_remote_copy(
            src_ref=own, dst_ref=every.at[f, s],
            send_sem=send2.at[df * n_space + ds], recv_sem=recv2.at[df * n_space + ds],
            device_id=at(df, ds), device_id_type=MESH,
        )
        copy.start()
        second.append(copy)
    every[f, s] = total
    for copy in second:
        copy.wait_recv()
    out_ref[...] = every[...]
    for copy in first + second:
        copy.wait_send()


def exchange(part, n_freq, n_space):
    piece = part.shape[1:]
    return pl.pallas_call(
        functools.partial(exchange_kernel, n_freq, n_space),
        out_shape=jax.ShapeDtypeStruct((n_freq, n_space) + piece, jnp.float32),
        in_specs=[pl.BlockSpec(memory_space=pltpu.VMEM)],
        out_specs=pl.BlockSpec(memory_space=pltpu.VMEM),
        scratch_shapes=[
            pltpu.VMEM((n_space,) + piece, jnp.float32),
            pltpu.VMEM(piece, jnp.float32),
            pltpu.VMEM((n_freq, n_space) + piece, jnp.float32),
            pltpu.SemaphoreType.DMA((n_space,)),
            pltpu.SemaphoreType.DMA((n_space,)),
            pltpu.SemaphoreType.DMA((n_freq * n_space,)),
            pltpu.SemaphoreType.DMA((n_freq * n_space,)),
        ],
        compiler_params=pltpu.CompilerParams(collective_id=0, has_side_effects=True),
        cost_estimate=pl.CostEstimate(flops=1 << 20, bytes_accessed=24 << 20, transcendentals=0),
        name="exchange",
    )(part)


def synthesis_kernel(factor, coef_ref, modes_ref, basis_ref, out_ref, left_ref, mid_ref):
    groups, _, blocks, half = coef_ref.shape
    parts, _, rows, tile = modes_ref.shape
    chunk = 2 * GROUP
    length = groups * GROUP

    @pl.when(pl.program_id(0) == 0)
    def _():
        lane = lax.broadcasted_iota(jnp.int32, (GROUP, 2 * half), 1) % half // (half // GROUP)
        mask = lane == lax.broadcasted_iota(jnp.int32, (GROUP, 2 * half), 0)

        def fill(g, carry):
            real = coef_ref[g, 0] * factor
            imag = coef_ref[g, 1] * factor
            line_r = jnp.concatenate([real, -imag], axis=1)
            line_i = jnp.concatenate([imag, real], axis=1)
            for b in range(blocks):
                left_ref[g, b * chunk : b * chunk + GROUP] = jnp.where(
                    mask, line_r[b : b + 1], 0.0
                ).astype(jnp.bfloat16)
                left_ref[g, b * chunk + GROUP : (b + 1) * chunk] = jnp.where(
                    mask, line_i[b : b + 1], 0.0
                ).astype(jnp.bfloat16)
            return carry

        lax.fori_loop(0, groups, fill, 0)

    for g in range(groups):
        pieces = []
        for c in range(2):
            start = g * half
            stop = start + half
            while start < stop:
                p, r = divmod(start, rows)
                n = min(stop - start, rows - r)
                pieces.append(modes_ref[p, c, r : r + n])
                start += n
        modes = jnp.concatenate(pieces, axis=0)
        rebuilt = jnp.dot(left_ref[g], modes, preferred_element_type=jnp.float32).astype(jnp.bfloat16)
        for b in range(blocks):
            mid_ref[b, g * chunk : (g + 1) * chunk] = rebuilt[b * chunk : (b + 1) * chunk]

    step = length // 2
    carry = None
    for b in range(blocks):
        series = jnp.dot(basis_ref[...], mid_ref[b], preferred_element_type=jnp.float32)
        lead = series[:step]
        out_ref[b * step : (b + 1) * step] = lead if carry is None else lead + carry
        carry = series[step:]
    out_ref[blocks * step :] = carry


def synthesis(coefs, modes, factor):
    groups, _, blocks, half = coefs.shape
    parts, _, rows, columns = modes.shape
    length = groups * GROUP
    tile = 256 if columns % 256 == 0 else columns
    freq = np.arange(length).reshape(groups, 1, GROUP)
    time = np.arange(length).reshape(length, 1, 1, 1)
    phase = 2.0 * np.pi * ((freq * time) % length) / length
    both = np.concatenate([np.cos(phase), -np.sin(phase)], axis=2)
    window = np.sin(np.pi * (np.arange(length) + 0.5) / length) / math.sqrt(length)
    basis = jnp.asarray((both.reshape(length, 2 * length) * window[:, None]).astype(np.float32)).astype(jnp.bfloat16)
    out_rows = (blocks + 1) * (length // 2)
    return pl.pallas_call(
        functools.partial(synthesis_kernel, factor),
        out_shape=jax.ShapeDtypeStruct((out_rows, columns), jnp.float32),
        grid=(columns // tile,),
        in_specs=[
            pl.BlockSpec((groups, 2, blocks, half), lambda i: (0, 0, 0, 0)),
            pl.BlockSpec((parts, 2, rows, tile), lambda i: (0, 0, 0, i)),
            pl.BlockSpec((length, 2 * length), lambda i: (0, 0)),
        ],
        out_specs=pl.BlockSpec((out_rows, tile), lambda i: (0, i)),
        scratch_shapes=[
            pltpu.VMEM((groups, blocks * 2 * GROUP, 2 * half), jnp.bfloat16),
            pltpu.VMEM((blocks, 2 * length, tile), jnp.bfloat16),
        ],
        compiler_params=pltpu.CompilerParams(vmem_limit_bytes=56 << 20),
        cost_estimate=pl.CostEstimate(
            flops=8 * length * length * blocks * columns, bytes_accessed=4 * out_rows * columns, transcendentals=0
        ),
        name="synthesis",
    )(coefs, modes, basis)


def body(spectra, eigvecs, weights):
    n_freq = lax.axis_size("freq")
    n_space = lax.axis_size("space")
    _, count, blocks, points = spectra.shape
    modes_count = eigvecs.shape[2]
    factor = 1.0 / math.sqrt(points * n_space)
    group = min(GROUP, count)
    width = points // n_freq
    send = eigvecs.reshape(2, count * modes_count, n_freq, width).transpose(2, 0, 1, 3)
    moved = lax.all_to_all(send, "freq", split_axis=0, concat_axis=0, tiled=True)
    part = project(
        send, spectra.reshape(2, count * blocks, points), weights.reshape(1, points), blocks, group, modes_count
    )
    piece = part.size // n_space
    shape = (piece // 128, 128) if piece % 128 == 0 else (1, piece)
    coefs = exchange(part.reshape((n_space,) + shape), n_freq, n_space)
    half = group * modes_count
    joined = GROUP // group
    coefs = coefs.reshape(-1, joined, 2, blocks, half).transpose(0, 2, 3, 1, 4)
    coefs = coefs.reshape(-1, 2, blocks, joined * half)
    return synthesis(coefs, moved, factor)


def solution(mesh):
    placed = (P(None, "freq", None, "space"), P(None, "freq", None, "space"), P("space"))
    return jax.shard_map(
        body, mesh=mesh, in_specs=placed, out_specs=P(None, ("space", "freq")), check_vma=False
    )
```

```python
import functools
import math

import jax
import jax.numpy as jnp
import numpy as np
from jax import lax
from jax.experimental import pallas as pl
from jax.experimental.pallas import tpu as pltpu
from jax.sharding import PartitionSpec as P


MESH = pl.DeviceIdType.MESH
GROUP = 32


def arrange_kernel(eigvecs_ref, *out_refs):
    _, count, modes_count, width = eigvecs_ref.shape
    rows = eigvecs_ref[0].reshape(count * modes_count, width)
    start = 0
    for out_ref in out_refs:
        stop = start + out_ref.shape[3]
        out_ref[0, 0] = rows[:, start:stop]
        start = stop


def arrange(eigvecs, parts, widths):
    _, count, modes_count, points = eigvecs.shape
    rows = count * modes_count
    return pl.pallas_call(
        arrange_kernel,
        out_shape=[jax.ShapeDtypeStruct((parts, 2, rows, w), eigvecs.dtype) for w in widths],
        grid=(parts, 2),
        in_specs=[pl.BlockSpec((1, count, modes_count, points // parts), lambda d, c: (c, 0, 0, d))],
        out_specs=[pl.BlockSpec((1, 1, rows, w), lambda d, c: (d, c, 0, 0)) for w in widths],
        compiler_params=pltpu.CompilerParams(vmem_limit_bytes=62 << 20),
        cost_estimate=pl.CostEstimate(flops=0, bytes_accessed=4 * eigvecs.size, transcendentals=0),
        name="arrange",
    )(eigvecs)


def project_kernel(blocks, group, spectra_ref, weights_ref, *refs):
    *modes_refs, out_ref, acc_ref = refs
    step = pl.program_id(1)
    half = modes_refs[0].shape[2]
    weights = weights_ref[...].astype(jnp.float32)
    weighted = jnp.concatenate(
        [
            (
                jnp.concatenate([ref[0, c] for ref in modes_refs], axis=1).astype(jnp.float32) * weights
            ).astype(jnp.bfloat16)
            for c in range(2)
        ],
        axis=0,
    )
    owner = lax.broadcasted_iota(jnp.int32, (blocks, 2 * half), 1) % half // (half // group)

    @pl.when(step == 0)
    def _():
        acc_ref[...] = jnp.zeros_like(acc_ref)

    for c in range(2):
        product = lax.dot_general(
            spectra_ref[c], weighted, (((1,), (1,)), ((), ())), preferred_element_type=jnp.float32
        )
        total = acc_ref[c]
        for j in range(group):
            total += jnp.where(owner == j, product[j * blocks : (j + 1) * blocks], 0.0)
        acc_ref[c] = total

    @pl.when(step == pl.num_programs(1) - 1)
    def _():
        out_ref[0, 0] = acc_ref[0][:, :half] + acc_ref[1][:, half:]
        out_ref[0, 1] = acc_ref[1][:, :half] - acc_ref[0][:, half:]


def project(modes, spectra, weights, blocks, group, modes_count):
    parts, _, rows, _ = modes[0].shape
    width = spectra.shape[2] // parts
    half = group * modes_count
    steps = rows // half
    points = spectra.shape[2]
    return pl.pallas_call(
        functools.partial(project_kernel, blocks, group),
        out_shape=jax.ShapeDtypeStruct((steps, 2, blocks, half), jnp.float32),
        grid=(steps, parts),
        in_specs=[
            pl.BlockSpec((2, group * blocks, width), lambda h, i: (0, h, i)),
            pl.BlockSpec((1, width), lambda h, i: (0, i)),
        ]
        + [pl.BlockSpec((1, 2, half, m.shape[3]), lambda h, i: (i, 0, h, 0)) for m in modes],
        out_specs=pl.BlockSpec((1, 2, blocks, half), lambda h, i: (h, 0, 0, 0)),
        scratch_shapes=[pltpu.VMEM((2, blocks, 2 * half), jnp.float32)],
        compiler_params=pltpu.CompilerParams(vmem_limit_bytes=62 << 20),
        cost_estimate=pl.CostEstimate(
            flops=4 * spectra.shape[1] * points * 2 * half,
            bytes_accessed=4 * spectra.shape[1] * points,
            transcendentals=0,
        ),
        name="project",
    )(spectra, weights, *modes)


def exchange_kernel(n_freq, n_space, part_ref, out_ref, land, own, every, send1, recv1, send2, recv2):
    f = lax.axis_index("freq")
    s = lax.axis_index("space")
    peers = [(df, ds) for df in range(n_freq) for ds in range(n_space) if (df, ds) != (0, 0)]

    def at(df, ds):
        return (lax.rem(f + df, n_freq), lax.rem(s + ds, n_space))

    barrier = pltpu.get_barrier_semaphore()
    for df, ds in peers:
        pl.semaphore_signal(barrier, inc=1, device_id=at(df, ds), device_id_type=MESH)
    pl.semaphore_wait(barrier, len(peers))

    first = []
    for ds in range(1, n_space):
        target = at(0, ds)
        copy = pltpu.make_async_remote_copy(
            src_ref=part_ref.at[target[1]], dst_ref=land.at[ds],
            send_sem=send1.at[ds], recv_sem=recv1.at[ds],
            device_id=target, device_id_type=MESH,
        )
        copy.start()
        first.append(copy)
    total = part_ref[s]
    for ds in range(1, n_space):
        first[ds - 1].wait_recv()
        total += land[ds]
    own[...] = total
    second = []
    for df, ds in peers:
        copy = pltpu.make_async_remote_copy(
            src_ref=own, dst_ref=every.at[f, s],
            send_sem=send2.at[df * n_space + ds], recv_sem=recv2.at[df * n_space + ds],
            device_id=at(df, ds), device_id_type=MESH,
        )
        copy.start()
        second.append(copy)
    every[f, s] = total
    for copy in second:
        copy.wait_recv()
    out_ref[...] = every[...]
    for copy in first + second:
        copy.wait_send()


def exchange(part, n_freq, n_space):
    piece = part.shape[1:]
    return pl.pallas_call(
        functools.partial(exchange_kernel, n_freq, n_space),
        out_shape=jax.ShapeDtypeStruct((n_freq, n_space) + piece, jnp.float32),
        in_specs=[pl.BlockSpec(memory_space=pltpu.VMEM)],
        out_specs=pl.BlockSpec(memory_space=pltpu.VMEM),
        scratch_shapes=[
            pltpu.VMEM((n_space,) + piece, jnp.float32),
            pltpu.VMEM(piece, jnp.float32),
            pltpu.VMEM((n_freq, n_space) + piece, jnp.float32),
            pltpu.SemaphoreType.DMA((n_space,)),
            pltpu.SemaphoreType.DMA((n_space,)),
            pltpu.SemaphoreType.DMA((n_freq * n_space,)),
            pltpu.SemaphoreType.DMA((n_freq * n_space,)),
        ],
        compiler_params=pltpu.CompilerParams(collective_id=0, has_side_effects=True),
        cost_estimate=pl.CostEstimate(flops=1 << 20, bytes_accessed=24 << 20, transcendentals=0),
        name="exchange",
    )(part)


def synthesis_kernel(factor, coef_ref, modes_ref, basis_ref, *refs):
    out_ref, left_ref, mid_ref = refs[-3:]
    groups, _, blocks, half = coef_ref.shape
    _, _, rows, _ = modes_ref.shape
    chunk = 2 * GROUP
    length = groups * GROUP

    @pl.when(pl.program_id(0) == 0)
    def _():
        lane = lax.broadcasted_iota(jnp.int32, (GROUP, 2 * half), 1) % half // (half // GROUP)
        mask = lane == lax.broadcasted_iota(jnp.int32, (GROUP, 2 * half), 0)

        def fill(g, carry):
            real = coef_ref[g, 0] * factor
            imag = coef_ref[g, 1] * factor
            line_r = jnp.concatenate([real, -imag], axis=1)
            line_i = jnp.concatenate([imag, real], axis=1)
            for b in range(blocks):
                left_ref[g, b * chunk : b * chunk + GROUP] = jnp.where(
                    mask, line_r[b : b + 1], 0.0
                ).astype(jnp.bfloat16)
                left_ref[g, b * chunk + GROUP : (b + 1) * chunk] = jnp.where(
                    mask, line_i[b : b + 1], 0.0
                ).astype(jnp.bfloat16)
            return carry

        lax.fori_loop(0, groups, fill, 0)

    for g in range(groups):
        pieces = []
        for c in range(2):
            start = g * half
            stop = start + half
            while start < stop:
                p, r = divmod(start, rows)
                n = min(stop - start, rows - r)
                pieces.append(modes_ref[p, c, r : r + n])
                start += n
        modes = jnp.concatenate(pieces, axis=0)
        rebuilt = jnp.dot(left_ref[g], modes, preferred_element_type=jnp.float32).astype(jnp.bfloat16)
        for b in range(blocks):
            mid_ref[b, g * chunk : (g + 1) * chunk] = rebuilt[b * chunk : (b + 1) * chunk]

    step = length // 2
    carry = None
    for b in range(blocks):
        series = jnp.dot(basis_ref[...], mid_ref[b], preferred_element_type=jnp.float32)
        lead = series[:step]
        out_ref[b * step : (b + 1) * step] = lead if carry is None else lead + carry
        carry = series[step:]
    out_ref[blocks * step :] = carry


def basis_of(groups):
    length = groups * GROUP
    freq = np.arange(length).reshape(groups, 1, GROUP)
    time = np.arange(length).reshape(length, 1, 1, 1)
    phase = 2.0 * np.pi * ((freq * time) % length) / length
    both = np.concatenate([np.cos(phase), -np.sin(phase)], axis=2)
    window = np.sin(np.pi * (np.arange(length) + 0.5) / length) / math.sqrt(length)
    return jnp.asarray((both.reshape(length, 2 * length) * window[:, None]).astype(np.float32)).astype(jnp.bfloat16)


def synthesis(coefs, modes, basis, factor, total, first, result):
    groups, _, blocks, half = coefs.shape
    parts, _, rows, columns = modes.shape
    length = groups * GROUP
    tile = 256 if columns % 256 == 0 else columns
    offset = first // tile
    out_rows = (blocks + 1) * (length // 2)
    earlier = [] if result is None else [result]
    return pl.pallas_call(
        functools.partial(synthesis_kernel, factor),
        out_shape=jax.ShapeDtypeStruct((out_rows, total), jnp.float32),
        grid=(columns // tile,),
        in_specs=[
            pl.BlockSpec((groups, 2, blocks, half), lambda i: (0, 0, 0, 0)),
            pl.BlockSpec((parts, 2, rows, tile), lambda i: (0, 0, 0, i)),
            pl.BlockSpec((length, 2 * length), lambda i: (0, 0)),
        ]
        + [pl.BlockSpec(memory_space=pl.ANY) for _ in earlier],
        out_specs=pl.BlockSpec((out_rows, tile), lambda i: (0, i + offset)),
        input_output_aliases={3: 0} if earlier else {},
        scratch_shapes=[
            pltpu.VMEM((groups, blocks * 2 * GROUP, 2 * half), jnp.bfloat16),
            pltpu.VMEM((blocks, 2 * length, tile), jnp.bfloat16),
        ],
        compiler_params=pltpu.CompilerParams(vmem_limit_bytes=40 << 20),
        cost_estimate=pl.CostEstimate(
            flops=8 * length * length * blocks * columns, bytes_accessed=4 * out_rows * columns, transcendentals=0
        ),
        name="synthesis",
    )(coefs, modes, basis, *earlier)


def body(spectra, eigvecs, weights):
    n_freq = lax.axis_size("freq")
    n_space = lax.axis_size("space")
    _, count, blocks, points = spectra.shape
    modes_count = eigvecs.shape[2]
    factor = 1.0 / math.sqrt(points * n_space)
    group = min(GROUP, count)
    width = points // n_freq
    if width % 512 == 0:
        widths = (width * 3 // 4, width // 4)
    else:
        widths = (width,)
    send = arrange(eigvecs, n_freq, widths)
    swap = functools.partial(lax.all_to_all, axis_name="freq", split_axis=0, concat_axis=0, tiled=True)
    moved = [swap(send[0])]
    spectra = spectra.reshape(2, count * blocks, points)
    weights = weights.reshape(1, points)
    part = project(send, spectra, weights, blocks, group, modes_count)
    piece = part.size // n_space
    shape = (piece // 128, 128) if piece % 128 == 0 else (1, piece)
    part = part.reshape((n_space,) + shape)
    coefs = exchange(part, n_freq, n_space)
    coefs, *later = lax.optimization_barrier((coefs, *send[1:]))
    moved += [swap(block) for block in later]
    half = group * modes_count
    joined = GROUP // group
    coefs = coefs.reshape(-1, joined, 2, blocks, half).transpose(0, 2, 3, 1, 4)
    coefs = coefs.reshape(-1, 2, blocks, joined * half)
    basis = basis_of(coefs.shape[0])
    result, first = None, 0
    for block in moved:
        result = synthesis(coefs, block, basis, factor, width, first, result)
        first += block.shape[3]
    return result


def solution(mesh):
    placed = (P(None, "freq", None, "space"), P(None, "freq", None, "space"), P("space"))
    return jax.shard_map(
        body, mesh=mesh, in_specs=placed, out_specs=P(None, ("space", "freq")), check_vma=False
    )
```
